128 devices in a mesh: sfc: 128 (over y, z, x, core).
Axes of the slice: x: 4, y: 4, z: 4, core: 2. Of those that a mesh axis runs over, the one named last changes fastest.
Arguments:
- state: float32 [5, 8192, 512], P(None, 'sfc'), may hold values from -0.47 to 4.3, as said below
- volume: int32 [8192, 512], P('sfc'), may hold values from 1 to 8, as said below
- neighbour: int32 [8192, 6], P('sfc'), may hold values from -1 to 8191, as said below
- parent: int32 [8192], P('sfc'), may hold values from 0 to 8191, as said below
Outputs:
- fine_state: float32 [5, 8192, 512], P(None, 'sfc')
- coarse_state: float32 [5, 1024, 512], P(None, 'sfc')
- coarse_residual: float32 [5, 1024, 512], P(None, 'sfc')
The draws below stay inside these ranges and needn't reach their ends.
Inputs may be any that keep to these rules, and one draw needn't show every extreme that they name: `state`: each cell has density 0.65 to 1.55, x velocity 0.2 to 0.8, y and z velocity of size 0.3 at most, pressure 0.55 to 1.45, and total energy = pressure / 0.4 + half the density times the squared speed. `volume`: every cell of a brick that is not cut holds 8; a cut brick has some cell under 8. One device's 64 bricks hold at most 16 cut bricks, and some device holds exactly 16. `neighbour`: the fine bricks form a grid of 32 x 16 x 16, periodic along y, with -1 on the far-field faces at the ends of x and z. The grid is cut into cubes of 4 x 4 x 4 bricks, ordered along a Morton curve: device d holds the cube whose coordinates (in cubes) have bit i // 3 of x, y or z equal to bit i of d, as i % 3 is 0, 1 or 2, as bricks d * 64 to (d + 1) * 64 - 1 in no particular order. The relation is symmetric. `parent`: every pair of a coarse brick and an octant occurs exactly once; the octant gives the parities of the fine brick's x, y and z positions. The coarse level is the fine grid halved, ordered along its own Morton curve and cut into runs of 8 that start half a run later than the fine level's cuts: coarse brick c is held by device c // 8, and of each device's fine bricks exactly 32 have their parents on the next device (the last device's on device 0) and the rest on the device itself.
All inputs are finite; a program needn't handle non-finite values.
Results may differ from the reference program's by a relative error of at most 0.00002.
Values sent between devices are 32-bit elements; how exact they have to be, the bound alone decides.
No kernel may reach another device: no remote copies, remote signals or barrier semaphores. Data moves between devices by JAX's collectives and lax.ppermute only.
A program may use at most 128 MiB of HBM per device.

```python
import jax
import jax.numpy as jnp
from jax import lax

BE = 8
CUBE = 4
GX = 32
GY = 16
GZ = 16
BRICK_DEV = 64
BRICKS = 8192
CBRICK_DEV = 8
CUT_MAX = 16


def random_orders(key, rows_count, length):
    return jax.vmap(lambda sub_key: jax.random.permutation(sub_key, length))(jax.random.split(key, rows_count)).astype(jnp.int32)


def alternate(coords, bit_total):
    result = jnp.zeros_like(coords[0])
    for position in range(bit_total):
        level_index = position // 3
        result = result + coords[position % 3] // 2 ** level_index % 2 * 2 ** position
    return result


def layout_tables(key):
    device_total = BRICKS // BRICK_DEV
    device_bits = device_total.bit_length() - 1
    cube_bits = CUBE.bit_length() - 1
    fine_perm = random_orders(jax.random.fold_in(key, 101), device_total, BRICK_DEV)
    coarse_perm = random_orders(jax.random.fold_in(key, 202), device_total, CBRICK_DEV)
    grid_shape = (GX, GY, GZ)
    x_grid = jnp.broadcast_to(jnp.arange(GX, dtype=jnp.int32)[:, None, None], grid_shape)
    y_grid = jnp.broadcast_to(jnp.arange(GY, dtype=jnp.int32)[None, :, None], grid_shape)
    z_grid = jnp.broadcast_to(jnp.arange(GZ, dtype=jnp.int32)[None, None, :], grid_shape)
    device_id = alternate((x_grid // CUBE, y_grid // CUBE, z_grid // CUBE), device_bits)
    local_id = alternate((x_grid % CUBE, y_grid % CUBE, z_grid % CUBE), 3 * cube_bits)
    brick_id = device_id * BRICK_DEV + fine_perm[device_id, local_id]
    entries = [jnp.where(x_grid > 0, jnp.roll(brick_id, 1, axis=0), -1), jnp.where(x_grid < GX - 1, jnp.roll(brick_id, -1, axis=0), -1), jnp.roll(brick_id, 1, axis=1), jnp.roll(brick_id, -1, axis=1), jnp.where(z_grid > 0, jnp.roll(brick_id, 1, axis=2), -1), jnp.where(z_grid < GZ - 1, jnp.roll(brick_id, -1, axis=2), -1)]
    flat_ids = brick_id.reshape(-1)
    neighbour_table = jnp.zeros((BRICKS, 6), jnp.int32).at[flat_ids].set(jnp.stack(entries, axis=-1).reshape(-1, 6).astype(jnp.int32))
    half_cube = CUBE // 2
    coarse_local = alternate((x_grid // 2 % half_cube, y_grid // 2 % half_cube, z_grid // 2 % half_cube), 3 * (cube_bits - 1))
    curve_pos = device_id * CBRICK_DEV + coarse_local + CBRICK_DEV // 2
    owner_dev = curve_pos // CBRICK_DEV % device_total
    coarse_id = owner_dev * CBRICK_DEV + coarse_perm[owner_dev, curve_pos % CBRICK_DEV]
    octant = (x_grid % 2 * 2 + y_grid % 2) * 2 + z_grid % 2
    parent_table = jnp.zeros((BRICKS,), jnp.int32).at[flat_ids].set((coarse_id * 8 + octant).reshape(-1).astype(jnp.int32))
    return (neighbour_table, parent_table)


def draw_neighbour(key, part):
    return layout_tables(key)[0]


def draw_parent(key, part):
    return layout_tables(key)[1]


def draw_volume(key, part):
    device_total = BRICKS // BRICK_DEV
    count_key, top_key, order_key, level_key, first_key = jax.random.split(jax.random.fold_in(key, 303), 5)
    cut_counts = jax.random.randint(count_key, (device_total,), 0, CUT_MAX + 1)
    busiest = jax.random.randint(top_key, (), 0, device_total)
    cut_counts = cut_counts.at[busiest].set(CUT_MAX)
    orders = random_orders(order_key, device_total, BRICK_DEV)
    is_cut = orders < cut_counts[:, None]
    levels = jax.random.randint(level_key, (device_total, BRICK_DEV, BE ** 3), 1, 9)
    first_cell = jax.random.randint(first_key, (device_total, BRICK_DEV), 1, 8)
    levels = levels.at[:, :, 0].set(first_cell)
    return jnp.where(is_cut[:, :, None], levels, 8).astype(jnp.int32).reshape(BRICKS, BE ** 3)


def draw_state(key, part):
    key_list = jax.random.split(jax.random.fold_in(key, 404), 5)
    grid_shape = (BRICKS, BE ** 3)
    density = 1.1 + 0.15 * jnp.clip(jax.random.normal(key_list[0], grid_shape, jnp.float32), -3.0, 3.0)
    speed_x = 0.5 + 0.1 * jnp.clip(jax.random.normal(key_list[1], grid_shape, jnp.float32), -3.0, 3.0)
    speed_y = 0.1 * jnp.clip(jax.random.normal(key_list[2], grid_shape, jnp.float32), -3.0, 3.0)
    speed_z = 0.1 * jnp.clip(jax.random.normal(key_list[3], grid_shape, jnp.float32), -3.0, 3.0)
    pressure = 1.0 + 0.15 * jnp.clip(jax.random.normal(key_list[4], grid_shape, jnp.float32), -3.0, 3.0)
    energy = pressure / 0.4 + 0.5 * density * (speed_x * speed_x + speed_y * speed_y + speed_z * speed_z)
    return jnp.stack([density, density * speed_x, density * speed_y, density * speed_z, energy]).astype(jnp.float32)


def setup_inputs(seed: int = 0) -> dict:
    splits = jax.random.split(jax.random.key(seed), 5)
    state = draw_state(jax.random.fold_in(splits[4], 71), 0)
    volume = draw_volume(jax.random.fold_in(splits[4], 71), 0)
    neighbour = draw_neighbour(jax.random.fold_in(splits[4], 71), 0)
    parent = draw_parent(jax.random.fold_in(splits[4], 71), 0)
    return {"state": state, "volume": volume, "neighbour": neighbour, "parent": parent}


HEAT_RATIO = 1.4
CFL_NUMBER = 0.25
FIRST_SECTION = 0.5

def free_stream():
    energy = 1.0 / (HEAT_RATIO * (HEAT_RATIO - 1.0)) + 0.125
    return jnp.array([1.0, 0.5, 0.0, 0.0, energy], dtype=jnp.float32)

def one_side(conserved, direction):
    density = conserved[0]
    velocity = conserved[1 + direction] / density
    kinetic = 0.5 * (conserved[1] * conserved[1] + conserved[2] * conserved[2] + conserved[3] * conserved[3]) / density
    pressure = (HEAT_RATIO - 1.0) * (conserved[4] - kinetic)
    sound_speed = jnp.sqrt(HEAT_RATIO * pressure / density)
    momenta = [conserved[1] * velocity, conserved[2] * velocity, conserved[3] * velocity]
    momenta[direction] = momenta[direction] + pressure
    fluxes = jnp.stack([conserved[1 + direction]] + momenta + [(conserved[4] + pressure) * velocity])
    return (fluxes, jnp.abs(velocity) + sound_speed)

def face_flux(left_state, right_state, direction):
    left_flux, left_speed = one_side(left_state, direction)
    right_flux, right_speed = one_side(right_state, direction)
    wave_speed = jnp.maximum(left_speed, right_speed)
    return (0.5 * (left_flux + right_flux) - 0.5 * wave_speed[None] * (right_state - left_state), wave_speed)

def evaluate(fields, fraction, ghost_state, ghost_fraction):
    residual = jnp.zeros_like(fields)
    spectral = jnp.zeros_like(fraction)
    for direction in range(3):
        state_dim = 2 + direction
        frac_dim = 1 + direction
        padded_state = jnp.concatenate([ghost_state[2 * direction], fields, ghost_state[2 * direction + 1]], axis=state_dim)
        padded_frac = jnp.concatenate([ghost_fraction[2 * direction], fraction, ghost_fraction[2 * direction + 1]], axis=frac_dim)
        extent = padded_state.shape[state_dim]
        left_state = lax.slice_in_dim(padded_state, 0, extent - 1, axis=state_dim)
        right_state = lax.slice_in_dim(padded_state, 1, extent, axis=state_dim)
        aperture = jnp.minimum(lax.slice_in_dim(padded_frac, 0, extent - 1, axis=frac_dim), lax.slice_in_dim(padded_frac, 1, extent, axis=frac_dim))
        fluxes, wave_speed = face_flux(left_state, right_state, direction)
        weighted = aperture[None] * fluxes
        spread = aperture * wave_speed
        residual = residual + lax.slice_in_dim(weighted, 1, extent - 1, axis=state_dim) - lax.slice_in_dim(weighted, 0, extent - 2, axis=state_dim)
        spectral = spectral + lax.slice_in_dim(spread, 1, extent - 1, axis=frac_dim) + lax.slice_in_dim(spread, 0, extent - 2, axis=frac_dim)
    return (residual, spectral)

def box_sum(values, first_dim):
    for offset in range(3):
        axis_dim = first_dim + offset
        extent = values.shape[axis_dim]
        widths = [(0, 0)] * values.ndim
        widths[axis_dim] = (1, 1)
        padded = jnp.pad(values, widths)
        values = lax.slice_in_dim(padded, 0, extent, axis=axis_dim) + lax.slice_in_dim(padded, 1, extent + 1, axis=axis_dim) + lax.slice_in_dim(padded, 2, extent + 2, axis=axis_dim)
    return values

def redistribute(increment, fraction):
    volume_share = fraction[None] * increment
    return volume_share + (1.0 - fraction[None]) * box_sum(volume_share, 2) / box_sum(fraction, 1)[None]

def octants(fields):
    half_edge = BE // 2
    row_count, bricks = (fields.shape[0], fields.shape[1])
    grouped = fields.reshape(row_count, bricks, half_edge, 2, half_edge, 2, half_edge, 2)
    return grouped.sum(axis=(3, 5, 7)).reshape(row_count, bricks, half_edge ** 3)

def assemble(placed):
    half_edge = BE // 2
    row_count, bricks = (placed.shape[0], placed.shape[1])
    grouped = placed.reshape(row_count, bricks, 2, 2, 2, half_edge, half_edge, half_edge)
    return grouped.transpose(0, 1, 2, 5, 3, 6, 4, 7).reshape(row_count, bricks, BE ** 3)

def layer_of(values, face_index, first_dim):
    position = BE - 1 if face_index % 2 == 0 else 0
    return lax.slice_in_dim(values, position, position + 1, axis=first_dim + face_index // 2)

def global_ghosts(fields, fraction, neighbour):
    stream = free_stream().reshape(5, 1, 1, 1, 1)
    ghost_state = []
    ghost_fraction = []
    for face_index in range(6):
        target = neighbour[:, face_index]
        present = target >= 0
        source_index = jnp.maximum(target, 0)
        fetched = jnp.take(layer_of(fields, face_index, 2), source_index, axis=1)
        fetched_frac = jnp.take(layer_of(fraction, face_index, 1), source_index, axis=0)
        ghost_state.append(jnp.where(present.reshape(1, -1, 1, 1, 1), fetched, stream))
        ghost_fraction.append(jnp.where(present.reshape(-1, 1, 1, 1), fetched_frac, layer_of(fraction, face_index ^ 1, 1)))
    return (ghost_state, ghost_fraction)

def section_terms(fields, fraction, neighbour, final):
    ghost_state, ghost_fraction = global_ghosts(fields, fraction, neighbour)
    pieces = [(fields, 1), (fraction, 0)] + [(ghost, 1) for ghost in ghost_state] + [(ghost, 0) for ghost in ghost_fraction]
    brick_total = fraction.shape[0]

    def block_step(index, result):
        start = (index * BRICK_DEV).astype(jnp.int32)
        taken_rows = [lax.dynamic_slice_in_dim(member, start, BRICK_DEV, member_dim) for member, member_dim in pieces]
        residual, spectral = evaluate(taken_rows[0], taken_rows[1], taken_rows[2:8], taken_rows[8:14])
        if final:
            update = residual
        else:
            update = redistribute(-CFL_NUMBER * residual / spectral[None], taken_rows[1])
        return lax.dynamic_update_slice_in_dim(result, update, start, 1)
    return lax.fori_loop(0, brick_total // BRICK_DEV, block_step, jnp.zeros_like(fields))

def reference(state, volume, neighbour, parent):
    brick_total = state.shape[1]
    fields = state.reshape(5, brick_total, BE, BE, BE)
    fraction = (volume.astype(jnp.float32) / 8.0).reshape(brick_total, BE, BE, BE)
    middle = fields + FIRST_SECTION * section_terms(fields, fraction, neighbour, False)
    fine_fields = fields + section_terms(middle, fraction, neighbour, False)
    fine_residual = section_terms(fine_fields, fraction, neighbour, True)
    octant_sums = jnp.concatenate([octants(fraction[None] * fine_fields), octants(fraction[None]), octants(fine_residual)], axis=0)
    placed = jnp.zeros((11, brick_total // 8, 8, octant_sums.shape[2]), jnp.float32).at[:, parent // 8, parent % 8].set(octant_sums)
    assembled = assemble(placed)
    return (fine_fields.reshape(5, brick_total, BE ** 3), assembled[0:5] / assembled[5:6], assembled[6:11])
```

```python
import jax
import jax.numpy as jnp
from jax import lax
from jax.experimental import pallas as pl
from jax.experimental.pallas import tpu as pltpu
from jax.sharding import PartitionSpec as P


ROWS = 256
LANES = 128
AXIS = "sfc"
HEAT_RATIO = 1.4
CFL_NUMBER = 0.25
FIRST_SECTION = 0.5
STREAM = (1.0, 0.5, 0.0, 0.0, 1.0 / (HEAT_RATIO * (HEAT_RATIO - 1.0)) + 0.125)
F32 = jnp.float32
BF16 = jnp.bfloat16
I32 = jnp.int32


def bits_of(direction, count):
    return [bit for bit in range(count.bit_length() - 1) if bit % 3 == direction]


def coordinates(device, count):
    return [
        sum((device >> bit & 1) << place for place, bit in enumerate(bits_of(direction, count)))
        for direction in range(3)
    ]


def pair_swaps(count):
    extents = [1 << len(bits_of(direction, count)) for direction in range(3)]
    number = {tuple(coordinates(device, count)): device for device in range(count)}
    swaps = []
    for direction in range(3):
        for other in (0, 1):
            pairs = []
            for device in range(count):
                place = coordinates(device, count)
                step = 1 if place[direction] % 2 == other else -1
                place[direction] = (place[direction] + step) % extents[direction]
                pairs.append((device, number[tuple(place)]))
            swaps.append(pairs)
    return swaps


def cube_place(device_ref, count):
    device = device_ref[0]
    place = coordinates(device, count)
    even = [place[direction] % 2 == 0 for direction in range(3)]
    far = [None, None, None]
    for direction in (0, 2):
        last = (1 << len(bits_of(direction, count))) - 1
        far[direction] = jnp.logical_or(place[direction] == 0, place[direction] == last)
    return device, even, far


def lane_index(shape=(8, LANES)):
    return lax.broadcasted_iota(I32, shape, len(shape) - 1)


def row_index(shape=(8, LANES)):
    return lax.broadcasted_iota(I32, shape, 0)


def turn(x, shift, axis):
    extent = x.shape[axis]
    shift = shift % extent
    return x if shift == 0 else pltpu.roll(x, shift, axis)


def place_of_register(i, iy):
    return pl.ds((i * 8 + iy) * 8, 8)


def slots():
    lane = lane_index()
    return lane & 7, lane >> 5, lane >> 3 & 3


LANE_STEP = (1, 32, 8)
EDGE = (7, 3, 3)
PACK = (8, 4, 4)


def layer_register(ref, lead, direction, side, number):
    if direction == 0:
        return ref[lead + (place_of_register(3 * side, number), slice(None))]
    if direction == 1:
        return ref[lead + (place_of_register(number, 7 * side), slice(None))]
    return ref[lead + (pl.ds(number * 64 + 7 * side, 8, stride=8), slice(None))]


def packed_layer(ref, lead, direction, side, slot):
    step, edge = LANE_STEP[direction], EDGE[direction] * side
    result = None
    for number in range(PACK[direction]):
        piece = turn(
            layer_register(ref, lead, direction, side, number), (number - edge) * step, 1
        )
        result = piece if result is None else jnp.where(slot == number, piece, result)
    return result


def write_messages(refs, message_refs, even):
    slot = slots()
    for variable, (ref, lead) in enumerate(refs):
        for direction in range(3):
            low = packed_layer(ref, lead, direction, 0, slot[direction])
            high = packed_layer(ref, lead, direction, 1, slot[direction])
            message_refs[2 * direction][variable] = jnp.where(even[direction], high, low)
            message_refs[2 * direction + 1][variable] = jnp.where(even[direction], low, high)


def primitives(conserved):
    density, mx, my, mz, energy = conserved
    inverse = 1.0 / density
    u, v, w = mx * inverse, my * inverse, mz * inverse
    pressure = (HEAT_RATIO - 1.0) * (energy - 0.5 * (mx * u + my * v + mz * w))
    sound = jnp.sqrt(HEAT_RATIO * pressure * inverse)
    return u, v, w, pressure, sound


def face_terms(left, right, aperture, direction, with_speed=True):
    ul, vl, pl_, cl = left
    ur, vr, pr, cr = right
    speed = jnp.maximum(jnp.abs(vl) + cl, jnp.abs(vr) + cr)
    half = 0.5 * aperture
    sums = [ul[1 + direction] + ur[1 + direction]]
    for momentum in (1, 2, 3):
        term = ul[momentum] * vl + ur[momentum] * vr
        if momentum == 1 + direction:
            term = term + (pl_ + pr)
        sums.append(term)
    sums.append((ul[4] + pl_) * vl + (ur[4] + pr) * vr)
    terms = [half * (sums[q] - speed * (ur[q] - ul[q])) for q in range(5)]
    if with_speed:
        terms.append(aperture * speed)
    return terms


def interior_body(u_ref, frac_ref, res_ref, prim_ref, wx_ref, with_speed):
    count = 6 if with_speed else 5
    sign = [-1.0] * 5 + [1.0]
    rows = row_index()
    slot = slots()
    for register in range(32):
        at = pl.ds(register * 8, 8)
        for q, value in enumerate(primitives([u_ref[q, at, :] for q in range(5)])):
            prim_ref[q, at, :] = value

    def cell(at, direction):
        return (
            [u_ref[q, at, :] for q in range(5)],
            prim_ref[direction, at, :],
            prim_ref[3, at, :],
            prim_ref[4, at, :],
        )

    def turned(side, shift, axis):
        return ([turn(x, shift, axis) for x in side[0]],) + tuple(
            turn(x, shift, axis) for x in side[1:]
        )

    def less(total, terms):
        return [total[q] - terms[q] if q < 5 else total[q] + terms[q] for q in range(count)]

    def plus(total, terms):
        return [total[q] + terms[q] for q in range(count)]

    for i in range(4):
        wy = None
        for iy in range(8):
            at = place_of_register(i, iy)
            frac = frac_ref[at, :]
            here = cell(at, 2)
            wz = face_terms(
                here,
                turned(here, -1, 0),
                jnp.where(rows == 7, 0.0, jnp.minimum(frac, turn(frac, -1, 0))),
                2,
                with_speed,
            )
            total = less(wz, [turn(x, 1, 0) for x in wz])
            if wy is not None:
                total = less(total, wy)
            if iy < 7:
                up = place_of_register(i, iy + 1)
                wy = face_terms(
                    cell(at, 1), cell(up, 1), jnp.minimum(frac, frac_ref[up, :]), 1, with_speed
                )
                total = plus(total, wy)
            if i > 0:
                total = less(total, [wx_ref[q, pl.ds(iy * 8, 8), :] for q in range(count)])
            if i < 3:
                up = place_of_register(i + 1, iy)
                wx = face_terms(
                    cell(at, 0), cell(up, 0), jnp.minimum(frac, frac_ref[up, :]), 0, with_speed
                )
                for q in range(count):
                    wx_ref[q, pl.ds(iy * 8, 8), :] = wx[q]
                total = plus(total, wx)
            for q in range(count):
                res_ref[q, at, :] = total[q]

    for direction in range(3):
        step = LANE_STEP[direction]
        for number in range(PACK[direction]):
            if direction == 0:
                top, bottom = place_of_register(3, number), place_of_register(0, number)
            elif direction == 1:
                top, bottom = place_of_register(number, 7), place_of_register(number, 0)
            else:
                top = pl.ds(number * 64 + 7, 8, stride=8)
                bottom = pl.ds(number * 64, 8, stride=8)
            aperture = jnp.where(
                slot[direction] == EDGE[direction],
                0.0,
                jnp.minimum(frac_ref[top, :], turn(frac_ref[bottom, :], -step, 1)),
            )
            terms = face_terms(
                cell(top, direction),
                turned(cell(bottom, direction), -step, 1),
                aperture,
                direction,
                with_speed,
            )
            for q in range(count):
                res_ref[q, top, :] = res_ref[q, top, :] + terms[q]
                back = turn(terms[q], step, 1)
                res_ref[q, bottom, :] = res_ref[q, bottom, :] + sign[q] * back


def boundary_body(
    res_ref, aperture_of, own_refs, ghost_refs, even, far, with_speed
):
    count = 6 if with_speed else 5
    slot = slots()
    for direction in range(3):
        terms = []
        for other in (0, 1):
            own_ref, ghost_ref = own_refs[2 * direction + other], ghost_refs[2 * direction + other]
            own = [own_ref[q] for q in range(5)]
            ghost = [ghost_ref[q] for q in range(5)]
            if other == 1 and far[direction] is not None:
                ghost = [jnp.where(far[direction], STREAM[q], ghost[q]) for q in range(5)]
            own_is_left = even[direction] if other == 0 else jnp.logical_not(even[direction])
            left = [jnp.where(own_is_left, own[q], ghost[q]) for q in range(5)]
            right = [jnp.where(own_is_left, ghost[q], own[q]) for q in range(5)]
            sides = []
            for values in (left, right):
                prims = primitives(values)
                sides.append((values, prims[direction], prims[3], prims[4]))
            terms.append(
                face_terms(sides[0], sides[1], aperture_of(direction, other), direction, with_speed)
            )
        step = LANE_STEP[direction]
        for q in range(count):
            high = jnp.where(even[direction], terms[0][q], terms[1][q])
            low = jnp.where(even[direction], terms[1][q], terms[0][q])
            for side, value in ((1, high), (0, low)):
                edge = EDGE[direction] * side
                for number in range(PACK[direction]):
                    if direction == 0:
                        at = place_of_register(3 * side, number)
                    elif direction == 1:
                        at = place_of_register(number, 7 * side)
                    else:
                        at = pl.ds(number * 64 + 7 * side, 8, stride=8)
                    piece = jnp.where(
                        slot[direction] == edge, turn(value, (edge - number) * step, 1), 0.0
                    )
                    if side == 0 and q < 5:
                        piece = -piece
                    res_ref[q, at, :] = res_ref[q, at, :] + piece


def box_sum(registers):
    rows = row_index()
    xs = slots()[0]
    result = []
    for i in range(4):
        along_z = [
            x
            + jnp.where(rows == 0, 0.0, turn(x, 1, 0))
            + jnp.where(rows == 7, 0.0, turn(x, -1, 0))
            for x in registers[i]
        ]
        along_y = []
        for iy in range(8):
            value = along_z[iy]
            if iy > 0:
                value = value + along_z[iy - 1]
            if iy < 7:
                value = value + along_z[iy + 1]
            along_y.append(value)
        result.append(along_y)
    boxed = [[None] * 8 for _ in range(4)]
    for iy in range(8):
        before = jnp.where(xs & 1 == 1, turn(result[3][iy], 1, 1), 0.0)
        after = jnp.where(xs & 1 == 0, turn(result[0][iy], -1, 1), 0.0)
        line = [before] + [result[i][iy] for i in range(4)] + [after]
        for i in range(4):
            boxed[i][iy] = line[i] + line[i + 1] + line[i + 2]
    return boxed


def split3(x):
    high = x.astype(BF16)
    rest = x - high.astype(F32)
    middle = rest.astype(BF16)
    low = (rest - middle.astype(F32)).astype(BF16)
    return high, middle, low


def as_column(row, count):
    same = row_index((count, count)) == lane_index((count, count))
    return jnp.sum(jnp.where(same, row, 0), axis=1, keepdims=True)


def brick_lane(device, neighbour_ref, parent_column):
    outside = (neighbour_ref[...] >> 6) != device
    outside = outside.astype(I32)
    place = []
    for direction in range(3):
        odd = parent_column >> (2 - direction) & 1
        upper = jnp.where(
            odd == 1,
            outside[:, 2 * direction + 1 : 2 * direction + 2],
            1 - outside[:, 2 * direction : 2 * direction + 1],
        )
        place.append(odd + 2 * upper)
    return place[1] * 32 + place[2] * 8 + place[0] * 2


def prepare_kernel(count, device_ref, state_ref, volume_ref, neighbour_ref, parent_ref, *outs):
    u_ref, frac_ref = outs[0:2]
    message_refs = outs[2:8]
    device, even, _ = cube_place(device_ref, count)
    lane = brick_lane(device, neighbour_ref, as_column(parent_ref[...], 64))
    spread = [
        (lane_index((64, LANES)) == lane + half).astype(F32).astype(BF16) for half in (0, 1)
    ]
    tripled = [jnp.concatenate([s, s, s], axis=0) for s in spread]
    dims = (((0,), (0,)), ((), ()))
    for q in range(5):
        parts = jnp.concatenate(split3(state_ref[q]), axis=0)
        u_ref[q] = lax.dot_general(
            parts[:, 0:256], tripled[0], dims, preferred_element_type=F32
        ) + lax.dot_general(parts[:, 256:512], tripled[1], dims, preferred_element_type=F32)
    volume = (volume_ref[...].astype(F32) / 8.0).astype(BF16)
    frac_ref[...] = lax.dot_general(
        volume[:, 0:256], spread[0], dims, preferred_element_type=F32
    ) + lax.dot_general(volume[:, 256:512], spread[1], dims, preferred_element_type=F32)
    write_messages([(u_ref, (q,)) for q in range(5)] + [(frac_ref, ())], message_refs, even)


def tables_kernel(count, device_ref, neighbour_ref, parent_ref, spread_ref, order_ref, pick_ref):
    device = device_ref[0]
    parent_row = parent_ref[...]
    parent_column = as_column(parent_row, 64)
    lane = brick_lane(device, neighbour_ref, parent_column)
    lanes = lane_index((64, LANES))
    spread = [(lanes == lane + half).astype(F32) for half in (0, 1)]
    spread_ref[0] = spread[0]
    spread_ref[1] = spread[1]
    slot = parent_column >> 3 & 7
    kept = (parent_column >> 6 == device).astype(I32)
    rank = []
    present_kept = None
    for flag in (kept, 1 - kept):
        present = jnp.max(
            jnp.where(lanes == slot, flag, 0), axis=0, keepdims=True
        )
        if present_kept is None:
            present_kept = present
        rank.append(jnp.sum(jnp.where(lanes < slot, present, 0), axis=1, keepdims=True))
    key = jnp.where(kept == 1, rank[0], 4 + rank[1]).astype(F32)
    key_row = jnp.sum((spread[0] + spread[1]) * key, axis=0, keepdims=True).astype(I32)
    lane_row = lane_index((1, LANES))
    half, lx, lz, ly = lane_row & 1, lane_row >> 1 & 3, lane_row >> 3 & 3, lane_row >> 5
    part = ((lx & 1) * 2 + half) * 4 + (ly & 1) * 2 + (lz & 1)
    order_ref[...] = (row_index((LANES, LANES)) == part * 8 + key_row).astype(F32)
    slots8, lanes8 = row_index(), lane_index()
    mine = jnp.sum(jnp.where(lanes8 == slots8, present_kept, 0), axis=1, keepdims=True)
    before = jnp.sum(jnp.where(lanes8 < slots8, present_kept, 0), axis=1, keepdims=True)
    source = jnp.where(mine == 1, before, 4 + slots8 - before)
    pick_ref[...] = (source == lanes8).astype(F32)


def mixing_kernel(frac_ref, mix_ref):
    frac = [[frac_ref[place_of_register(i, iy), :] for iy in range(8)] for i in range(4)]
    boxed = box_sum(frac)
    for i in range(4):
        for iy in range(8):
            mix_ref[place_of_register(i, iy), :] = (1.0 - frac[i][iy]) / boxed[i][iy]


def interior_kernel(with_speed, u_ref, frac_ref, res_ref, prim_ref, wx_ref):
    interior_body(u_ref, frac_ref, res_ref, prim_ref, wx_ref, with_speed)


def update_kernel(count, first, device_ref, *refs):
    base_ref, frac_ref, mix_ref, inner_ref = refs[0:4]
    own_refs, ghost_refs = refs[4:10], refs[10:16]
    refs = refs[16:]
    if first:
        new_ref, message_refs, faces_ref, res_ref = refs[0], refs[1:7], refs[7], refs[8]
    else:
        faces_ref, new_ref, message_refs, res_ref = refs[0], refs[1], refs[2:8], refs[8]
    _, even, far = cube_place(device_ref, count)
    res_ref[...] = inner_ref[...]

    def aperture_of(direction, other):
        number = 2 * direction + other
        if not first:
            return faces_ref[number]
        own, ghost = own_refs[number][5], ghost_refs[number][5]
        if other == 1 and far[direction] is not None:
            ghost = jnp.where(far[direction], own, ghost)
        aperture = jnp.minimum(own, ghost)
        faces_ref[number] = aperture
        return aperture

    boundary_body(res_ref, aperture_of, own_refs, ghost_refs, even, far, True)
    for register in range(32):
        at = pl.ds(register * 8, 8)
        scale = frac_ref[at, :] * (-CFL_NUMBER / res_ref[5, at, :])
        for q in range(5):
            res_ref[q, at, :] = res_ref[q, at, :] * scale
    factor = FIRST_SECTION if first else 1.0
    for q in range(5):
        share = [[res_ref[q, place_of_register(i, iy), :] for iy in range(8)] for i in range(4)]
        boxed = box_sum(share)
        for i in range(4):
            for iy in range(8):
                at = place_of_register(i, iy)
                mixed = share[i][iy] + mix_ref[at, :] * boxed[i][iy]
                if first:
                    mixed = factor * mixed
                new_ref[q, at, :] = base_ref[q, at, :] + mixed
    write_messages([(new_ref, (q,)) for q in range(5)], message_refs, even)


def coarse_rows(registers, order3, rows_ref, half_ref):
    for i in (0, 1):
        for jy in range(4):
            half_ref[pl.ds((i * 4 + jy) * 8, 8), :] = (
                registers(2 * i, 2 * jy)
                + registers(2 * i, 2 * jy + 1)
                + registers(2 * i + 1, 2 * jy)
                + registers(2 * i + 1, 2 * jy + 1)
            )
    for i in (0, 1):
        for jy in range(4):
            start = (i * 4 + jy) * 8
            rows_ref[pl.ds(i * 64 + jy * 8, 4), :] = (
                half_ref[pl.ds(start, 4, stride=2), :] + half_ref[pl.ds(start + 1, 4, stride=2), :]
            )
    parts = jnp.concatenate(split3(rows_ref[...]), axis=1)
    placed = lax.dot_general(order3, parts, (((1,), (1,)), ((), ())), preferred_element_type=F32)
    tiles = []
    for tile in range(4):
        total = None
        for number in range(4):
            start = (tile * 4 + number) * 8
            piece = turn(placed[start : start + 8, :], (number // 2) * 32 + (number % 2) * 4, 1)
            total = piece if total is None else total + piece
        tiles.append(total)
    return jnp.concatenate(tiles, axis=1)


def tripled_order(order_ref):
    order = order_ref[...].astype(BF16)
    return jnp.concatenate([order, order, order], axis=1)


def state_kernel(u_ref, frac_ref, spread_ref, order_ref, out_ref, kept_ref, sent_ref, rows_ref, half_ref):
    rows_ref[...] = jnp.zeros_like(rows_ref)
    tripled = []
    for half in (0, 1):
        spread = spread_ref[half].astype(BF16)
        tripled.append(jnp.concatenate([spread, spread, spread], axis=1))
    order3 = tripled_order(order_ref)
    dims = (((1,), (1,)), ((), ()))
    for q in range(5):
        parts = jnp.concatenate(split3(u_ref[q]), axis=1)
        for half in (0, 1):
            out_ref[q, :, pl.ds(half * 256, 256)] = lax.dot_general(
                tripled[half], parts, dims, preferred_element_type=F32
            )
    for q in range(6):
        if q < 5:
            def registers(i, iy, q=q):
                at = place_of_register(i, iy)
                return frac_ref[at, :] * u_ref[q, at, :]
        else:
            def registers(i, iy):
                return frac_ref[place_of_register(i, iy), :]
        sums = coarse_rows(registers, order3, rows_ref, half_ref)
        kept_ref[q] = sums[0:4]
        sent_ref[q] = sums[4:8]


def residual_kernel(count, device_ref, *refs):
    inner_ref, faces_ref, order_ref = refs[0:3]
    own_refs, ghost_refs = refs[3:9], refs[9:15]
    kept_ref, sent_ref, res_ref, rows_ref, half_ref = refs[15:20]
    _, even, far = cube_place(device_ref, count)
    res_ref[...] = inner_ref[...]
    boundary_body(
        res_ref,
        lambda direction, other: faces_ref[2 * direction + other],
        own_refs,
        ghost_refs,
        even,
        far,
        False,
    )
    rows_ref[...] = jnp.zeros_like(rows_ref)
    order3 = tripled_order(order_ref)
    for q in range(5):
        sums = coarse_rows(
            lambda i, iy: res_ref[q, place_of_register(i, iy), :], order3, rows_ref, half_ref
        )
        kept_ref[q] = sums[0:4]
        sent_ref[q] = sums[4:8]


def coarse_kernel(pick_ref, kept_state_ref, kept_res_ref, state_ref, res_ref, out_state_ref, out_res_ref):
    pick = pick_ref[...]

    def choose(kept, received):
        result = None
        for source in range(8):
            row = kept[source : source + 1] if source < 4 else received[source - 4 : source - 3]
            piece = jnp.where(pick[:, source : source + 1] > 0.5, row, 0.0)
            result = piece if result is None else result + piece
        return result

    weight = choose(kept_state_ref[5], state_ref[5])
    for q in range(5):
        out_state_ref[q] = choose(kept_state_ref[q], state_ref[q]) / weight
        out_res_ref[q] = choose(kept_res_ref[q], res_ref[q])


def f32(*shape):
    return jax.ShapeDtypeStruct(shape, F32)


def call(kernel, outs, scratch, args, name, smem=1):
    vmem = pl.BlockSpec(memory_space=pltpu.VMEM)
    specs = [pl.BlockSpec(memory_space=pltpu.SMEM)] * smem + [vmem] * (len(args) - smem)
    return pl.pallas_call(
        kernel,
        out_shape=outs,
        in_specs=specs,
        out_specs=[vmem] * len(outs),
        scratch_shapes=[pltpu.VMEM(shape, F32) for shape in scratch],
        name=name,
        cost_estimate=pl.CostEstimate(flops=8_000_000, bytes_accessed=4_000_000, transcendentals=0),
    )(*args)


def solution(mesh):
    count = mesh.shape[AXIS]
    swaps = pair_swaps(count)
    forward = [(device, (device + 1) % count) for device in range(count)]

    def exchange(messages):
        ghosts = [None] * 6
        for number in (5, 3, 1, 4, 2, 0):
            ghosts[number] = lax.ppermute(messages[number], AXIS, swaps[number])
        return ghosts

    def interior(u, frac, with_speed, name):
        rows = 6 if with_speed else 5
        return call(
            lambda *refs: interior_kernel(with_speed, *refs),
            [f32(rows, ROWS, LANES)],
            [(5, ROWS, LANES), (rows, 64, LANES)],
            [u, frac],
            name,
            0,
        )[0]

    def local(state, volume, neighbour, parent):
        device = lax.axis_index(AXIS).astype(I32).reshape(1)
        parent = parent.reshape(1, 64)
        grid = f32(5, ROWS, LANES)
        u, frac, *sent = call(
            lambda *refs: prepare_kernel(count, *refs),
            [grid, f32(ROWS, LANES)] + [f32(6, 8, LANES)] * 6,
            [],
            [device, state, volume, neighbour, parent],
            "prepare",
        )
        ghosts = exchange(sent)
        spread, order, pick = call(
            lambda *refs: tables_kernel(count, *refs),
            [f32(2, 64, LANES), f32(LANES, LANES), f32(8, LANES)],
            [],
            [device, neighbour, parent],
            "tables",
        )
        mix = call(mixing_kernel, [f32(ROWS, LANES)], [], [frac], "mixing", 0)[0]
        inner = interior(u, frac, True, "interior_1")
        middle, *rest = call(
            lambda *refs: update_kernel(count, True, *refs),
            [grid] + [f32(5, 8, LANES)] * 6 + [f32(6, 8, LANES)],
            [(6, ROWS, LANES)],
            [device, u, frac, mix, inner, *sent, *ghosts],
            "update_1",
        )
        sent, faces = rest[0:6], rest[6]
        ghosts = exchange(sent)
        inner = interior(middle, frac, True, "interior_2")
        fine, *sent = call(
            lambda *refs: update_kernel(count, False, *refs),
            [grid] + [f32(5, 8, LANES)] * 6,
            [(6, ROWS, LANES)],
            [device, u, frac, mix, inner, *sent, *ghosts, faces],
            "update_2",
        )
        ghosts = exchange(sent)
        inner = interior(fine, frac, False, "interior_3")
        fine_out, kept_state, sent_state = call(
            state_kernel,
            [f32(5, 64, 512), f32(6, 4, 512), f32(6, 4, 512)],
            [(LANES, LANES), (64, LANES)],
            [fine, frac, spread, order],
            "restrict_state",
            0,
        )
        kept_res, sent_res = call(
            lambda *refs: residual_kernel(count, *refs),
            [f32(5, 4, 512), f32(5, 4, 512)],
            [(5, ROWS, LANES), (LANES, LANES), (64, LANES)],
            [device, inner, faces, order, *sent, *ghosts],
            "restrict_residual",
        )
        got_state = lax.ppermute(sent_state, AXIS, forward)
        got_res = lax.ppermute(sent_res, AXIS, forward)
        coarse_state, coarse_residual = call(
            coarse_kernel,
            [f32(5, 8, 512), f32(5, 8, 512)],
            [],
            [pick, kept_state, kept_res, got_state, got_res],
            "coarse",
            0,
        )
        return fine_out, coarse_state, coarse_residual

    in_specs = (P(None, AXIS, None), P(AXIS, None), P(AXIS, None), P(AXIS))
    out_specs = (P(None, AXIS, None), P(None, AXIS, None), P(None, AXIS, None))
    return jax.shard_map(local, mesh=mesh, in_specs=in_specs, out_specs=out_specs, check_vma=False)
```

```python
import jax
import jax.numpy as jnp
from jax import lax
from jax.experimental import pallas as pl
from jax.experimental.pallas import tpu as pltpu
from jax.sharding import PartitionSpec as P


ROWS = 256
LANES = 128
AXIS = "sfc"
HEAT_RATIO = 1.4
CFL_NUMBER = 0.25
FIRST_SECTION = 0.5
STREAM = (1.0, 0.5, 0.0, 0.0, 1.0 / (HEAT_RATIO * (HEAT_RATIO - 1.0)) + 0.125)
F32 = jnp.float32
BF16 = jnp.bfloat16
I32 = jnp.int32


def bits_of(direction, count):
    return [bit for bit in range(count.bit_length() - 1) if bit % 3 == direction]


def coordinates(device, count):
    return [
        sum((device >> bit & 1) << place for place, bit in enumerate(bits_of(direction, count)))
        for direction in range(3)
    ]


def pair_swaps(count):
    extents = [1 << len(bits_of(direction, count)) for direction in range(3)]
    number = {tuple(coordinates(device, count)): device for device in range(count)}
    swaps = []
    for direction in range(3):
        for other in (0, 1):
            pairs = []
            for device in range(count):
                place = coordinates(device, count)
                step = 1 if place[direction] % 2 == other else -1
                place[direction] = (place[direction] + step) % extents[direction]
                pairs.append((device, number[tuple(place)]))
            swaps.append(pairs)
    return swaps


def cube_place(device_ref, count):
    device = device_ref[0]
    place = coordinates(device, count)
    even = [place[direction] % 2 == 0 for direction in range(3)]
    far = [None, None, None]
    for direction in (0, 2):
        last = (1 << len(bits_of(direction, count))) - 1
        far[direction] = jnp.logical_or(place[direction] == 0, place[direction] == last)
    return device, even, far


def lane_index(shape=(8, LANES)):
    return lax.broadcasted_iota(I32, shape, len(shape) - 1)


def row_index(shape=(8, LANES)):
    return lax.broadcasted_iota(I32, shape, 0)


def turn(x, shift, axis):
    extent = x.shape[axis]
    shift = shift % extent
    return x if shift == 0 else pltpu.roll(x, shift, axis)


def place_of_register(i, iy):
    return pl.ds((i * 8 + iy) * 8, 8)


def slots():
    lane = lane_index()
    return lane & 7, lane >> 5, lane >> 3 & 3


LANE_STEP = (1, 32, 8)
EDGE = (7, 3, 3)
PACK = (8, 4, 4)


def layer_register(ref, lead, direction, side, number):
    if direction == 0:
        return ref[lead + (place_of_register(3 * side, number), slice(None))]
    if direction == 1:
        return ref[lead + (place_of_register(number, 7 * side), slice(None))]
    return ref[lead + (pl.ds(number * 64 + 7 * side, 8, stride=8), slice(None))]


def packed_layer(ref, lead, direction, side, slot):
    step, edge = LANE_STEP[direction], EDGE[direction] * side
    result = None
    for number in range(PACK[direction]):
        piece = turn(
            layer_register(ref, lead, direction, side, number), (number - edge) * step, 1
        )
        result = piece if result is None else jnp.where(slot == number, piece, result)
    return result


def write_messages(refs, message_refs, even):
    slot = slots()
    for variable, (ref, lead) in enumerate(refs):
        for direction in range(3):
            low = packed_layer(ref, lead, direction, 0, slot[direction])
            high = packed_layer(ref, lead, direction, 1, slot[direction])
            message_refs[2 * direction][variable] = jnp.where(even[direction], high, low)
            message_refs[2 * direction + 1][variable] = jnp.where(even[direction], low, high)


def primitives(conserved):
    density, mx, my, mz, energy = conserved
    inverse = 1.0 / density
    u, v, w = mx * inverse, my * inverse, mz * inverse
    pressure = (HEAT_RATIO - 1.0) * (energy - 0.5 * (mx * u + my * v + mz * w))
    sound = jnp.sqrt(HEAT_RATIO * pressure * inverse)
    return u, v, w, pressure, sound


def face_terms(left, right, aperture, direction, with_speed=True):
    ul, vl, pl_, cl = left
    ur, vr, pr, cr = right
    speed = jnp.maximum(jnp.abs(vl) + cl, jnp.abs(vr) + cr)
    half = 0.5 * aperture
    sums = [ul[1 + direction] + ur[1 + direction]]
    for momentum in (1, 2, 3):
        term = ul[momentum] * vl + ur[momentum] * vr
        if momentum == 1 + direction:
            term = term + (pl_ + pr)
        sums.append(term)
    sums.append((ul[4] + pl_) * vl + (ur[4] + pr) * vr)
    terms = [half * (sums[q] - speed * (ur[q] - ul[q])) for q in range(5)]
    if with_speed:
        terms.append(aperture * speed)
    return terms


def interior_body(u_ref, frac_ref, res_ref, prim_ref, wx_ref, with_speed):
    count = 6 if with_speed else 5
    sign = [-1.0] * 5 + [1.0]
    rows = row_index()
    slot = slots()
    for register in range(32):
        at = pl.ds(register * 8, 8)
        for q, value in enumerate(primitives([u_ref[q, at, :] for q in range(5)])):
            prim_ref[q, at, :] = value

    def cell(at, direction):
        return (
            [u_ref[q, at, :] for q in range(5)],
            prim_ref[direction, at, :],
            prim_ref[3, at, :],
            prim_ref[4, at, :],
        )

    def turned(side, shift, axis):
        return ([turn(x, shift, axis) for x in side[0]],) + tuple(
            turn(x, shift, axis) for x in side[1:]
        )

    def less(total, terms):
        return [total[q] - terms[q] if q < 5 else total[q] + terms[q] for q in range(count)]

    def plus(total, terms):
        return [total[q] + terms[q] for q in range(count)]

    for i in range(4):
        wy = None
        for iy in range(8):
            at = place_of_register(i, iy)
            frac = frac_ref[at, :]
            here = cell(at, 2)
            wz = face_terms(
                here,
                turned(here, -1, 0),
                jnp.where(rows == 7, 0.0, jnp.minimum(frac, turn(frac, -1, 0))),
                2,
                with_speed,
            )
            total = less(wz, [turn(x, 1, 0) for x in wz])
            if wy is not None:
                total = less(total, wy)
            if iy < 7:
                up = place_of_register(i, iy + 1)
                wy = face_terms(
                    cell(at, 1), cell(up, 1), jnp.minimum(frac, frac_ref[up, :]), 1, with_speed
                )
                total = plus(total, wy)
            if i > 0:
                total = less(total, [wx_ref[q, pl.ds(iy * 8, 8), :] for q in range(count)])
            if i < 3:
                up = place_of_register(i + 1, iy)
                wx = face_terms(
                    cell(at, 0), cell(up, 0), jnp.minimum(frac, frac_ref[up, :]), 0, with_speed
                )
                for q in range(count):
                    wx_ref[q, pl.ds(iy * 8, 8), :] = wx[q]
                total = plus(total, wx)
            for q in range(count):
                res_ref[q, at, :] = total[q]

    for direction in range(3):
        step = LANE_STEP[direction]
        for number in range(PACK[direction]):
            if direction == 0:
                top, bottom = place_of_register(3, number), place_of_register(0, number)
            elif direction == 1:
                top, bottom = place_of_register(number, 7), place_of_register(number, 0)
            else:
                top = pl.ds(number * 64 + 7, 8, stride=8)
                bottom = pl.ds(number * 64, 8, stride=8)
            aperture = jnp.where(
                slot[direction] == EDGE[direction],
                0.0,
                jnp.minimum(frac_ref[top, :], turn(frac_ref[bottom, :], -step, 1)),
            )
            terms = face_terms(
                cell(top, direction),
                turned(cell(bottom, direction), -step, 1),
                aperture,
                direction,
                with_speed,
            )
            for q in range(count):
                res_ref[q, top, :] = res_ref[q, top, :] + terms[q]
                back = turn(terms[q], step, 1)
                res_ref[q, bottom, :] = res_ref[q, bottom, :] + sign[q] * back


def boundary_body(
    res_ref, aperture_of, own_refs, ghost_refs, even, far, with_speed
):
    count = 6 if with_speed else 5
    slot = slots()
    for direction in range(3):
        terms = []
        for other in (0, 1):
            own_ref, ghost_ref = own_refs[2 * direction + other], ghost_refs[2 * direction + other]
            own = [own_ref[q] for q in range(5)]
            ghost = [ghost_ref[q] for q in range(5)]
            if other == 1 and far[direction] is not None:
                ghost = [jnp.where(far[direction], STREAM[q], ghost[q]) for q in range(5)]
            own_is_left = even[direction] if other == 0 else jnp.logical_not(even[direction])
            left = [jnp.where(own_is_left, own[q], ghost[q]) for q in range(5)]
            right = [jnp.where(own_is_left, ghost[q], own[q]) for q in range(5)]
            sides = []
            for values in (left, right):
                prims = primitives(values)
                sides.append((values, prims[direction], prims[3], prims[4]))
            terms.append(
                face_terms(sides[0], sides[1], aperture_of(direction, other), direction, with_speed)
            )
        step = LANE_STEP[direction]
        for q in range(count):
            high = jnp.where(even[direction], terms[0][q], terms[1][q])
            low = jnp.where(even[direction], terms[1][q], terms[0][q])
            for side, value in ((1, high), (0, low)):
                edge = EDGE[direction] * side
                for number in range(PACK[direction]):
                    if direction == 0:
                        at = place_of_register(3 * side, number)
                    elif direction == 1:
                        at = place_of_register(number, 7 * side)
                    else:
                        at = pl.ds(number * 64 + 7 * side, 8, stride=8)
                    piece = jnp.where(
                        slot[direction] == edge, turn(value, (edge - number) * step, 1), 0.0
                    )
                    if side == 0 and q < 5:
                        piece = -piece
                    res_ref[q, at, :] = res_ref[q, at, :] + piece


def box_sum(registers):
    rows = row_index()
    xs = slots()[0]
    result = []
    for i in range(4):
        along_z = [
            x
            + jnp.where(rows == 0, 0.0, turn(x, 1, 0))
            + jnp.where(rows == 7, 0.0, turn(x, -1, 0))
            for x in registers[i]
        ]
        along_y = []
        for iy in range(8):
            value = along_z[iy]
            if iy > 0:
                value = value + along_z[iy - 1]
            if iy < 7:
                value = value + along_z[iy + 1]
            along_y.append(value)
        result.append(along_y)
    boxed = [[None] * 8 for _ in range(4)]
    for iy in range(8):
        before = jnp.where(xs & 1 == 1, turn(result[3][iy], 1, 1), 0.0)
        after = jnp.where(xs & 1 == 0, turn(result[0][iy], -1, 1), 0.0)
        line = [before] + [result[i][iy] for i in range(4)] + [after]
        for i in range(4):
            boxed[i][iy] = line[i] + line[i + 1] + line[i + 2]
    return boxed


def split3(x):
    high = x.astype(BF16)
    rest = x - high.astype(F32)
    middle = rest.astype(BF16)
    low = (rest - middle.astype(F32)).astype(BF16)
    return high, middle, low


def as_column(row, count):
    same = row_index((count, count)) == lane_index((count, count))
    return jnp.sum(jnp.where(same, row, 0), axis=1, keepdims=True)


def brick_lane(device, neighbour, parent):
    outside = ((neighbour >> 6) != device).astype(I32)
    place = []
    for direction in range(3):
        odd = parent >> (2 - direction) & 1
        upper = jnp.where(
            odd == 1,
            outside[2 * direction + 1 : 2 * direction + 2],
            1 - outside[2 * direction : 2 * direction + 1],
        )
        place.append(odd + 2 * upper)
    return place[1] * 32 + place[2] * 8 + place[0] * 2


def prepare_kernel(count, device_ref, state_hbm, volume_hbm, neighbour_hbm, parent_hbm, *refs):
    u_ref, frac_ref = refs[0:2]
    message_refs = refs[2:8]
    state_ref, volume_ref, neighbour_ref, parent_ref, sems = refs[8:13]
    copies = [
        pltpu.make_async_copy(neighbour_hbm, neighbour_ref, sems.at[0]),
        pltpu.make_async_copy(parent_hbm, parent_ref, sems.at[1]),
        pltpu.make_async_copy(volume_hbm, volume_ref, sems.at[2]),
    ]
    for q in range(5):
        copies.append(pltpu.make_async_copy(state_hbm.at[q], state_ref.at[q], sems.at[3 + q]))
    for copy in copies:
        copy.start()
    device, even, _ = cube_place(device_ref, count)
    copies[0].wait()
    copies[1].wait()
    lane = as_column(brick_lane(device, neighbour_ref[...], parent_ref[...]), 64)
    spread = [
        (lane_index((64, LANES)) == lane + half).astype(F32).astype(BF16) for half in (0, 1)
    ]
    tripled = [jnp.concatenate([s, s, s], axis=0) for s in spread]
    dims = (((0,), (0,)), ((), ()))
    copies[2].wait()
    volume = (volume_ref[...].astype(F32) / 8.0).astype(BF16)
    frac_ref[...] = lax.dot_general(
        volume[:, 0:256], spread[0], dims, preferred_element_type=F32
    ) + lax.dot_general(volume[:, 256:512], spread[1], dims, preferred_element_type=F32)
    for q in range(5):
        copies[3 + q].wait()
        parts = jnp.concatenate(split3(state_ref[q]), axis=0)
        u_ref[q] = lax.dot_general(
            parts[:, 0:256], tripled[0], dims, preferred_element_type=F32
        ) + lax.dot_general(parts[:, 256:512], tripled[1], dims, preferred_element_type=F32)
    write_messages([(u_ref, (q,)) for q in range(5)] + [(frac_ref, ())], message_refs, even)


def tables_kernel(device_ref, neighbour_ref, parent_ref, spread_ref, order_ref, pick_ref):
    device = device_ref[0]
    parent_column = as_column(parent_ref[...], 64)
    lane = as_column(brick_lane(device, neighbour_ref[...], parent_ref[...]), 64)
    lanes = lane_index((64, LANES))
    spread = [(lanes == lane + half).astype(F32) for half in (0, 1)]
    spread_ref[0] = spread[0]
    spread_ref[1] = spread[1]
    slot = parent_column >> 3 & 7
    kept = (parent_column >> 6 == device).astype(I32)
    rank = []
    present_kept = None
    for flag in (kept, 1 - kept):
        present = jnp.max(
            jnp.where(lanes == slot, flag, 0), axis=0, keepdims=True
        )
        if present_kept is None:
            present_kept = present
        rank.append(jnp.sum(jnp.where(lanes < slot, present, 0), axis=1, keepdims=True))
    key = jnp.where(kept == 1, rank[0], 4 + rank[1]).astype(F32)
    key_row = jnp.sum((spread[0] + spread[1]) * key, axis=0, keepdims=True).astype(I32)
    lane_row = lane_index((1, LANES))
    half, lx, lz, ly = lane_row & 1, lane_row >> 1 & 3, lane_row >> 3 & 3, lane_row >> 5
    part = ((lx & 1) * 2 + half) * 4 + (ly & 1) * 2 + (lz & 1)
    order_ref[...] = (row_index((LANES, LANES)) == part * 8 + key_row).astype(F32)
    slots8, lanes8 = row_index(), lane_index()
    mine = jnp.sum(jnp.where(lanes8 == slots8, present_kept, 0), axis=1, keepdims=True)
    before = jnp.sum(jnp.where(lanes8 < slots8, present_kept, 0), axis=1, keepdims=True)
    source = jnp.where(mine == 1, before, 4 + slots8 - before)
    pick_ref[...] = (source == lanes8).astype(F32)


def mixing_kernel(frac_ref, mix_ref):
    frac = [[frac_ref[place_of_register(i, iy), :] for iy in range(8)] for i in range(4)]
    boxed = box_sum(frac)
    for i in range(4):
        for iy in range(8):
            mix_ref[place_of_register(i, iy), :] = (1.0 - frac[i][iy]) / boxed[i][iy]


def interior_kernel(with_speed, u_ref, frac_ref, res_ref, prim_ref, wx_ref):
    interior_body(u_ref, frac_ref, res_ref, prim_ref, wx_ref, with_speed)


def update_kernel(count, first, device_ref, *refs):
    base_ref, frac_ref, mix_ref, inner_ref = refs[0:4]
    own_refs, ghost_refs = refs[4:10], refs[10:16]
    refs = refs[16:]
    if first:
        new_ref, message_refs, faces_ref, res_ref = refs[0], refs[1:7], refs[7], refs[8]
    else:
        faces_ref, new_ref, message_refs, res_ref = refs[0], refs[1], refs[2:8], refs[8]
    _, even, far = cube_place(device_ref, count)
    res_ref[...] = inner_ref[...]

    def aperture_of(direction, other):
        number = 2 * direction + other
        if not first:
            return faces_ref[number]
        own, ghost = own_refs[number][5], ghost_refs[number][5]
        if other == 1 and far[direction] is not None:
            ghost = jnp.where(far[direction], own, ghost)
        aperture = jnp.minimum(own, ghost)
        faces_ref[number] = aperture
        return aperture

    boundary_body(res_ref, aperture_of, own_refs, ghost_refs, even, far, True)
    for register in range(32):
        at = pl.ds(register * 8, 8)
        scale = frac_ref[at, :] * (-CFL_NUMBER / res_ref[5, at, :])
        for q in range(5):
            res_ref[q, at, :] = res_ref[q, at, :] * scale
    factor = FIRST_SECTION if first else 1.0
    for q in range(5):
        share = [[res_ref[q, place_of_register(i, iy), :] for iy in range(8)] for i in range(4)]
        boxed = box_sum(share)
        for i in range(4):
            for iy in range(8):
                at = place_of_register(i, iy)
                mixed = share[i][iy] + mix_ref[at, :] * boxed[i][iy]
                if first:
                    mixed = factor * mixed
                new_ref[q, at, :] = base_ref[q, at, :] + mixed
    write_messages([(new_ref, (q,)) for q in range(5)], message_refs, even)


def coarse_rows(registers, order3, rows_ref, half_ref):
    for i in (0, 1):
        for jy in range(4):
            half_ref[pl.ds((i * 4 + jy) * 8, 8), :] = (
                registers(2 * i, 2 * jy)
                + registers(2 * i, 2 * jy + 1)
                + registers(2 * i + 1, 2 * jy)
                + registers(2 * i + 1, 2 * jy + 1)
            )
    for i in (0, 1):
        for jy in range(4):
            start = (i * 4 + jy) * 8
            rows_ref[pl.ds(i * 64 + jy * 8, 4), :] = (
                half_ref[pl.ds(start, 4, stride=2), :] + half_ref[pl.ds(start + 1, 4, stride=2), :]
            )
    parts = jnp.concatenate(split3(rows_ref[...]), axis=1)
    placed = lax.dot_general(order3, parts, (((1,), (1,)), ((), ())), preferred_element_type=F32)
    tiles = []
    for tile in range(4):
        total = None
        for number in range(4):
            start = (tile * 4 + number) * 8
            piece = turn(placed[start : start + 8, :], (number // 2) * 32 + (number % 2) * 4, 1)
            total = piece if total is None else total + piece
        tiles.append(total)
    return jnp.concatenate(tiles, axis=1)


def tripled_order(order_ref):
    order = order_ref[...].astype(BF16)
    return jnp.concatenate([order, order, order], axis=1)


def state_kernel(u_ref, frac_ref, order_ref, kept_ref, sent_ref, rows_ref, half_ref):
    rows_ref[...] = jnp.zeros_like(rows_ref)
    order3 = tripled_order(order_ref)
    for q in range(6):
        if q < 5:
            def registers(i, iy, q=q):
                at = place_of_register(i, iy)
                return frac_ref[at, :] * u_ref[q, at, :]
        else:
            def registers(i, iy):
                return frac_ref[place_of_register(i, iy), :]
        sums = coarse_rows(registers, order3, rows_ref, half_ref)
        kept_ref[q] = sums[0:4]
        sent_ref[q] = sums[4:8]


def output_kernel(u_ref, spread_ref, out_ref):
    tripled = []
    for half in (0, 1):
        spread = spread_ref[half].astype(BF16)
        tripled.append(jnp.concatenate([spread, spread, spread], axis=1))
    dims = (((1,), (1,)), ((), ()))
    for q in range(5):
        parts = jnp.concatenate(split3(u_ref[q]), axis=1)
        for half in (0, 1):
            out_ref[q, :, pl.ds(half * 256, 256)] = lax.dot_general(
                tripled[half], parts, dims, preferred_element_type=F32
            )


def residual_kernel(count, device_ref, *refs):
    inner_ref, faces_ref, order_ref, sent_state_ref = refs[0:4]
    own_refs, ghost_refs = refs[4:10], refs[10:16]
    kept_ref, sent_ref, res_ref, rows_ref, half_ref = refs[16:21]
    _, even, far = cube_place(device_ref, count)
    res_ref[...] = inner_ref[...]
    boundary_body(
        res_ref,
        lambda direction, other: faces_ref[2 * direction + other],
        own_refs,
        ghost_refs,
        even,
        far,
        False,
    )
    rows_ref[...] = jnp.zeros_like(rows_ref)
    order3 = tripled_order(order_ref)
    for q in range(5):
        sums = coarse_rows(
            lambda i, iy: res_ref[q, place_of_register(i, iy), :], order3, rows_ref, half_ref
        )
        kept_ref[q] = sums[0:4]
        sent_ref[6 + q] = sums[4:8]
    sent_ref[0:6] = sent_state_ref[...]


def coarse_kernel(pick_ref, kept_state_ref, kept_res_ref, got_ref, out_state_ref, out_res_ref):
    pick = pick_ref[...]
    chosen = [jnp.broadcast_to(pick[:, source : source + 1], (8, 512)) > 0.5 for source in range(8)]

    def choose(kept, received):
        result = None
        for source in range(8):
            row = kept[source : source + 1] if source < 4 else received[source - 4 : source - 3]
            row = jnp.broadcast_to(row, (8, 512))
            result = row if result is None else jnp.where(chosen[source], row, result)
        return result

    weight = choose(kept_state_ref[5], got_ref[5])
    for q in range(5):
        out_state_ref[q] = choose(kept_state_ref[q], got_ref[q]) / weight
        out_res_ref[q] = choose(kept_res_ref[q], got_ref[6 + q])


def f32(*shape):
    return jax.ShapeDtypeStruct(shape, F32)


def held(*shape):
    return pltpu.VMEM(shape, F32)


def call(kernel, outs, scratch, args, smem=1, sources=0):
    vmem = pl.BlockSpec(memory_space=pltpu.VMEM)
    spaces = [pltpu.SMEM] * smem + [pltpu.HBM] * sources
    spaces += [pltpu.VMEM] * (len(args) - len(spaces))
    args = [
        pltpu.with_memory_space_constraint(arg, space) if space is not pltpu.SMEM else arg
        for arg, space in zip(args, spaces)
    ]
    return pl.pallas_call(
        kernel,
        out_shape=outs,
        in_specs=[pl.BlockSpec(memory_space=space) for space in spaces],
        out_specs=[vmem] * len(outs),
        scratch_shapes=[pltpu.VMEM(item, F32) if isinstance(item, tuple) else item for item in scratch],
        compiler_params=pltpu.CompilerParams(vmem_limit_bytes=8 << 20),
        cost_estimate=pl.CostEstimate(flops=8_000_000, bytes_accessed=4_000_000, transcendentals=0),
    )(*args)


START_ORDER = (5, 3, 1, 4, 2, 0)


def solution(mesh):
    count = mesh.shape[AXIS]
    swaps = pair_swaps(count)
    forward = [(device, (device + 1) % count) for device in range(count)]

    def exchange(messages):
        ghosts = [None] * 6
        for number in START_ORDER:
            ghosts[number] = lax.ppermute(messages[number], AXIS, swaps[number])
        return ghosts

    def interior(u, frac, with_speed):
        rows = 6 if with_speed else 5
        return call(
            lambda *refs: interior_kernel(with_speed, *refs),
            [held(rows, ROWS, LANES)],
            [(5, ROWS, LANES), (rows, 64, LANES)],
            [u, frac],
            0,
        )[0]

    def local(state, volume, neighbour, parent):
        device = lax.axis_index(AXIS).astype(I32).reshape(1)
        parent = parent.reshape(1, 64)
        neighbour = neighbour.T
        grid = held(5, ROWS, LANES)
        u, frac, *sent = call(
            lambda *refs: prepare_kernel(count, *refs),
            [grid, held(ROWS, LANES)] + [held(6, 8, LANES)] * 6,
            [
                (5, 64, 512),
                pltpu.VMEM((64, 512), I32),
                pltpu.VMEM((6, 64), I32),
                pltpu.VMEM((1, 64), I32),
                pltpu.SemaphoreType.DMA((8,)),
            ],
            [device, state, volume, neighbour, parent],
            1,
            4,
        )
        ghosts = exchange(sent)
        spread, order, pick = call(
            lambda *refs: tables_kernel(*refs),
            [held(2, 64, LANES), held(LANES, LANES), held(8, LANES)],
            [],
            [device, neighbour, parent],
        )
        mix = call(mixing_kernel, [held(ROWS, LANES)], [], [frac], 0)[0]
        inner = interior(u, frac, True)
        middle, *rest = call(
            lambda *refs: update_kernel(count, True, *refs),
            [grid] + [held(5, 8, LANES)] * 6 + [held(6, 8, LANES)],
            [(6, ROWS, LANES)],
            [device, u, frac, mix, inner, *sent, *ghosts],
        )
        sent, faces = rest[0:6], rest[6]
        ghosts = exchange(sent)
        inner = interior(middle, frac, True)
        fine, *sent = call(
            lambda *refs: update_kernel(count, False, *refs),
            [grid] + [held(5, 8, LANES)] * 6,
            [(6, ROWS, LANES)],
            [device, u, frac, mix, inner, *sent, *ghosts, faces],
        )
        ghosts = exchange(sent)
        inner = interior(fine, frac, False)
        kept_state, sent_state = call(
            state_kernel,
            [held(6, 4, 512), held(6, 4, 512)],
            [(LANES, LANES), (64, LANES)],
            [fine, frac, order],
            0,
        )
        kept_res, outgoing = call(
            lambda *refs: residual_kernel(count, *refs),
            [held(5, 4, 512), held(11, 4, 512)],
            [(5, ROWS, LANES), (LANES, LANES), (64, LANES)],
            [device, inner, faces, order, sent_state, *sent, *ghosts],
        )
        got = lax.ppermute(outgoing, AXIS, forward)
        fine_out = call(output_kernel, [f32(5, 64, 512)], [], [fine, spread], 0)[0]
        coarse_state, coarse_residual = call(
            coarse_kernel,
            [f32(5, 8, 512), f32(5, 8, 512)],
            [],
            [pick, kept_state, kept_res, got],
            0,
        )
        return fine_out, coarse_state, coarse_residual

    in_specs = (P(None, AXIS, None), P(AXIS, None), P(AXIS, None), P(AXIS))
    out_specs = (P(None, AXIS, None), P(None, AXIS, None), P(None, AXIS, None))
    return jax.shard_map(local, mesh=mesh, in_specs=in_specs, out_specs=out_specs, check_vma=False)
```

```python
import jax
import jax.numpy as jnp
from jax import lax
from jax.experimental import pallas as pl
from jax.experimental.pallas import tpu as pltpu
from jax.sharding import PartitionSpec as P


ROWS = 256
LANES = 128
AXIS = "sfc"
HEAT_RATIO = 1.4
CFL_NUMBER = 0.25
FIRST_SECTION = 0.5
STREAM = (1.0, 0.5, 0.0, 0.0, 1.0 / (HEAT_RATIO * (HEAT_RATIO - 1.0)) + 0.125)
F32 = jnp.float32
BF16 = jnp.bfloat16
I32 = jnp.int32


def bits_of(direction, count):
    return [bit for bit in range(count.bit_length() - 1) if bit % 3 == direction]


def coordinates(device, count):
    return [
        sum((device >> bit & 1) << place for place, bit in enumerate(bits_of(direction, count)))
        for direction in range(3)
    ]


def pair_swaps(count):
    extents = [1 << len(bits_of(direction, count)) for direction in range(3)]
    number = {tuple(coordinates(device, count)): device for device in range(count)}
    swaps = []
    for direction in range(3):
        for other in (0, 1):
            pairs = []
            for device in range(count):
                place = coordinates(device, count)
                step = 1 if place[direction] % 2 == other else -1
                there = place[direction] + step
                if direction == 1 or 0 <= there < extents[direction]:
                    place[direction] = there % extents[direction]
                else:
                    place[1 if direction == 0 else 0] ^= 1
                pairs.append((device, number[tuple(place)]))
            swaps.append(pairs)
    return swaps


def cube_place(count):
    device = lax.axis_index(AXIS)
    place = coordinates(device, count)
    even = [place[direction] % 2 == 0 for direction in range(3)]
    far = [None, None, None]
    for direction in (0, 2):
        last = (1 << len(bits_of(direction, count))) - 1
        far[direction] = jnp.logical_or(place[direction] == 0, place[direction] == last)
    return device, even, far


def lane_index(shape=(8, LANES)):
    return lax.broadcasted_iota(I32, shape, len(shape) - 1)


def row_index(shape=(8, LANES)):
    return lax.broadcasted_iota(I32, shape, 0)


def turn(x, shift, axis):
    extent = x.shape[axis]
    shift = shift % extent
    return x if shift == 0 else pltpu.roll(x, shift, axis)


def place_of_register(i, iy):
    return pl.ds((i * 8 + iy) * 8, 8)


def slots():
    lane = lane_index()
    return lane & 7, lane >> 5, lane >> 3 & 3


LANE_STEP = (1, 32, 8)
EDGE = (7, 3, 3)
PACK = (8, 4, 4)


def layer_register(ref, lead, direction, side, number):
    if direction == 0:
        return ref[lead + (place_of_register(3 * side, number), slice(None))]
    if direction == 1:
        return ref[lead + (place_of_register(number, 7 * side), slice(None))]
    return ref[lead + (pl.ds(number * 64 + 7 * side, 8, stride=8), slice(None))]


def packed_layer(ref, lead, direction, side, slot):
    step, edge = LANE_STEP[direction], EDGE[direction] * side
    result = None
    for number in range(PACK[direction]):
        piece = turn(
            layer_register(ref, lead, direction, side, number), (number - edge) * step, 1
        )
        result = piece if result is None else jnp.where(slot == number, piece, result)
    return result


def write_messages(refs, message_refs, even):
    slot = slots()
    for variable, (ref, lead) in enumerate(refs):
        for direction in range(3):
            low = packed_layer(ref, lead, direction, 0, slot[direction])
            high = packed_layer(ref, lead, direction, 1, slot[direction])
            message_refs[2 * direction][variable] = jnp.where(even[direction], high, low)
            message_refs[2 * direction + 1][variable] = jnp.where(even[direction], low, high)


def primitives(conserved):
    density, mx, my, mz, energy = conserved
    inverse = 1.0 / density
    u, v, w = mx * inverse, my * inverse, mz * inverse
    pressure = (HEAT_RATIO - 1.0) * (energy - 0.5 * (mx * u + my * v + mz * w))
    sound = jnp.sqrt(HEAT_RATIO * pressure * inverse)
    return u, v, w, pressure, sound


def face_terms(left, right, aperture, direction, with_speed=True):
    ul, vl, pl_, cl = left
    ur, vr, pr, cr = right
    speed = jnp.maximum(jnp.abs(vl) + cl, jnp.abs(vr) + cr)
    half = 0.5 * aperture
    sums = [ul[1 + direction] + ur[1 + direction]]
    for momentum in (1, 2, 3):
        term = ul[momentum] * vl + ur[momentum] * vr
        if momentum == 1 + direction:
            term = term + (pl_ + pr)
        sums.append(term)
    sums.append((ul[4] + pl_) * vl + (ur[4] + pr) * vr)
    terms = [half * (sums[q] - speed * (ur[q] - ul[q])) for q in range(5)]
    if with_speed:
        terms.append(aperture * speed)
    return terms


def interior_body(u_ref, frac_ref, res_ref, prim_ref, wx_ref, with_speed):
    count = 6 if with_speed else 5
    sign = [-1.0] * 5 + [1.0]
    rows = row_index()
    slot = slots()
    for register in range(32):
        at = pl.ds(register * 8, 8)
        for q, value in enumerate(primitives([u_ref[q, at, :] for q in range(5)])):
            prim_ref[q, at, :] = value

    def cell(at, direction):
        return (
            [u_ref[q, at, :] for q in range(5)],
            prim_ref[direction, at, :],
            prim_ref[3, at, :],
            prim_ref[4, at, :],
        )

    def turned(side, shift, axis):
        return ([turn(x, shift, axis) for x in side[0]],) + tuple(
            turn(x, shift, axis) for x in side[1:]
        )

    def less(total, terms):
        return [total[q] - terms[q] if q < 5 else total[q] + terms[q] for q in range(count)]

    def plus(total, terms):
        return [total[q] + terms[q] for q in range(count)]

    for i in range(4):
        wy = None
        for iy in range(8):
            at = place_of_register(i, iy)
            frac = frac_ref[at, :]
            here = cell(at, 2)
            wz = face_terms(
                here,
                turned(here, -1, 0),
                jnp.where(rows == 7, 0.0, jnp.minimum(frac, turn(frac, -1, 0))),
                2,
                with_speed,
            )
            total = less(wz, [turn(x, 1, 0) for x in wz])
            if wy is not None:
                total = less(total, wy)
            if iy < 7:
                up = place_of_register(i, iy + 1)
                wy = face_terms(
                    cell(at, 1), cell(up, 1), jnp.minimum(frac, frac_ref[up, :]), 1, with_speed
                )
                total = plus(total, wy)
            if i > 0:
                total = less(total, [wx_ref[q, pl.ds(iy * 8, 8), :] for q in range(count)])
            if i < 3:
                up = place_of_register(i + 1, iy)
                wx = face_terms(
                    cell(at, 0), cell(up, 0), jnp.minimum(frac, frac_ref[up, :]), 0, with_speed
                )
                for q in range(count):
                    wx_ref[q, pl.ds(iy * 8, 8), :] = wx[q]
                total = plus(total, wx)
            for q in range(count):
                res_ref[q, at, :] = total[q]

    for direction in range(3):
        step = LANE_STEP[direction]
        for number in range(PACK[direction]):
            if direction == 0:
                top, bottom = place_of_register(3, number), place_of_register(0, number)
            elif direction == 1:
                top, bottom = place_of_register(number, 7), place_of_register(number, 0)
            else:
                top = pl.ds(number * 64 + 7, 8, stride=8)
                bottom = pl.ds(number * 64, 8, stride=8)
            aperture = jnp.where(
                slot[direction] == EDGE[direction],
                0.0,
                jnp.minimum(frac_ref[top, :], turn(frac_ref[bottom, :], -step, 1)),
            )
            terms = face_terms(
                cell(top, direction),
                turned(cell(bottom, direction), -step, 1),
                aperture,
                direction,
                with_speed,
            )
            for q in range(count):
                res_ref[q, top, :] = res_ref[q, top, :] + terms[q]
                back = turn(terms[q], step, 1)
                res_ref[q, bottom, :] = res_ref[q, bottom, :] + sign[q] * back


def boundary_body(
    res_ref, aperture_of, own_refs, ghost_refs, even, far, with_speed
):
    count = 6 if with_speed else 5
    slot = slots()
    for direction in range(3):
        terms = []
        for other in (0, 1):
            own_ref, ghost_ref = own_refs[2 * direction + other], ghost_refs[2 * direction + other]
            own = [own_ref[q] for q in range(5)]
            ghost = [ghost_ref[q] for q in range(5)]
            if other == 1 and far[direction] is not None:
                ghost = [jnp.where(far[direction], STREAM[q], ghost[q]) for q in range(5)]
            own_is_left = even[direction] if other == 0 else jnp.logical_not(even[direction])
            left = [jnp.where(own_is_left, own[q], ghost[q]) for q in range(5)]
            right = [jnp.where(own_is_left, ghost[q], own[q]) for q in range(5)]
            sides = []
            for values in (left, right):
                prims = primitives(values)
                sides.append((values, prims[direction], prims[3], prims[4]))
            terms.append(
                face_terms(sides[0], sides[1], aperture_of(direction, other), direction, with_speed)
            )
        step = LANE_STEP[direction]
        for q in range(count):
            high = jnp.where(even[direction], terms[0][q], terms[1][q])
            low = jnp.where(even[direction], terms[1][q], terms[0][q])
            for side, value in ((1, high), (0, low)):
                edge = EDGE[direction] * side
                for number in range(PACK[direction]):
                    if direction == 0:
                        at = place_of_register(3 * side, number)
                    elif direction == 1:
                        at = place_of_register(number, 7 * side)
                    else:
                        at = pl.ds(number * 64 + 7 * side, 8, stride=8)
                    piece = jnp.where(
                        slot[direction] == edge, turn(value, (edge - number) * step, 1), 0.0
                    )
                    if side == 0 and q < 5:
                        piece = -piece
                    res_ref[q, at, :] = res_ref[q, at, :] + piece


def box_sum(registers):
    rows = row_index()
    xs = slots()[0]
    result = []
    for i in range(4):
        along_z = [
            x
            + jnp.where(rows == 0, 0.0, turn(x, 1, 0))
            + jnp.where(rows == 7, 0.0, turn(x, -1, 0))
            for x in registers[i]
        ]
        along_y = []
        for iy in range(8):
            value = along_z[iy]
            if iy > 0:
                value = value + along_z[iy - 1]
            if iy < 7:
                value = value + along_z[iy + 1]
            along_y.append(value)
        result.append(along_y)
    boxed = [[None] * 8 for _ in range(4)]
    for iy in range(8):
        before = jnp.where(xs & 1 == 1, turn(result[3][iy], 1, 1), 0.0)
        after = jnp.where(xs & 1 == 0, turn(result[0][iy], -1, 1), 0.0)
        line = [before] + [result[i][iy] for i in range(4)] + [after]
        for i in range(4):
            boxed[i][iy] = line[i] + line[i + 1] + line[i + 2]
    return boxed


def split3(x):
    high = x.astype(BF16)
    rest = x - high.astype(F32)
    middle = rest.astype(BF16)
    low = (rest - middle.astype(F32)).astype(BF16)
    return high, middle, low


def as_column(row, count):
    same = row_index((count, count)) == lane_index((count, count))
    return jnp.sum(jnp.where(same, row, 0), axis=1, keepdims=True)


def brick_lane(device, neighbour, parent):
    outside = ((neighbour >> 6) != device).astype(I32)
    place = []
    for direction in range(3):
        odd = parent >> (2 - direction) & 1
        upper = jnp.where(
            odd == 1,
            outside[2 * direction + 1 : 2 * direction + 2],
            1 - outside[2 * direction : 2 * direction + 1],
        )
        place.append(odd + 2 * upper)
    return place[1] * 32 + place[2] * 8 + place[0] * 2


def prepare_kernel(count, state_hbm, volume_hbm, neighbour_hbm, parent_hbm, *refs):
    u_ref, frac_ref = refs[0:2]
    message_refs = refs[2:8]
    state_ref, volume_ref, neighbour_ref, parent_ref, sems = refs[8:13]
    copies = [
        pltpu.make_async_copy(neighbour_hbm, neighbour_ref, sems.at[0]),
        pltpu.make_async_copy(parent_hbm, parent_ref, sems.at[1]),
        pltpu.make_async_copy(volume_hbm, volume_ref, sems.at[2]),
    ]
    for q in range(5):
        copies.append(pltpu.make_async_copy(state_hbm.at[q], state_ref.at[q], sems.at[3 + q]))
    for copy in copies:
        copy.start()
    device, even, _ = cube_place(count)
    copies[0].wait()
    copies[1].wait()
    lane = as_column(brick_lane(device, neighbour_ref[...], parent_ref[...]), 64)
    spread = [
        (lane_index((64, LANES)) == lane + half).astype(F32).astype(BF16) for half in (0, 1)
    ]
    tripled = [jnp.concatenate([s, s, s], axis=0) for s in spread]
    dims = (((0,), (0,)), ((), ()))
    copies[2].wait()
    volume = (volume_ref[...].astype(F32) / 8.0).astype(BF16)
    frac_ref[...] = lax.dot_general(
        volume[:, 0:256], spread[0], dims, preferred_element_type=F32
    ) + lax.dot_general(volume[:, 256:512], spread[1], dims, preferred_element_type=F32)
    for q in range(5):
        copies[3 + q].wait()
        parts = jnp.concatenate(split3(state_ref[q]), axis=0)
        u_ref[q] = lax.dot_general(
            parts[:, 0:256], tripled[0], dims, preferred_element_type=F32
        ) + lax.dot_general(parts[:, 256:512], tripled[1], dims, preferred_element_type=F32)
    write_messages([(u_ref, (q,)) for q in range(5)] + [(frac_ref, ())], message_refs, even)


def tables_kernel(neighbour_ref, parent_ref, spread_ref, order_ref, pick_ref):
    device = lax.axis_index(AXIS)
    parent_column = as_column(parent_ref[...], 64)
    lane = as_column(brick_lane(device, neighbour_ref[...], parent_ref[...]), 64)
    lanes = lane_index((64, LANES))
    spread = [(lanes == lane + half).astype(F32) for half in (0, 1)]
    spread_ref[0] = spread[0]
    spread_ref[1] = spread[1]
    slot = parent_column >> 3 & 7
    kept = (parent_column >> 6 == device).astype(I32)
    rank = []
    present_kept = None
    for flag in (kept, 1 - kept):
        present = jnp.max(
            jnp.where(lanes == slot, flag, 0), axis=0, keepdims=True
        )
        if present_kept is None:
            present_kept = present
        rank.append(jnp.sum(jnp.where(lanes < slot, present, 0), axis=1, keepdims=True))
    key = jnp.where(kept == 1, rank[0], 4 + rank[1]).astype(F32)
    key_row = jnp.sum((spread[0] + spread[1]) * key, axis=0, keepdims=True).astype(I32)
    lane_row = lane_index((1, LANES))
    half, lx, lz, ly = lane_row & 1, lane_row >> 1 & 3, lane_row >> 3 & 3, lane_row >> 5
    part = ((lx & 1) * 2 + half) * 4 + (ly & 1) * 2 + (lz & 1)
    order_ref[...] = (row_index((LANES, LANES)) == part * 8 + key_row).astype(F32)
    slots8, lanes8 = row_index(), lane_index()
    mine = jnp.sum(jnp.where(lanes8 == slots8, present_kept, 0), axis=1, keepdims=True)
    before = jnp.sum(jnp.where(lanes8 < slots8, present_kept, 0), axis=1, keepdims=True)
    source = jnp.where(mine == 1, before, 4 + slots8 - before)
    pick_ref[...] = (source == lanes8).astype(F32)


def mixing_kernel(frac_ref, mix_ref):
    frac = [[frac_ref[place_of_register(i, iy), :] for iy in range(8)] for i in range(4)]
    boxed = box_sum(frac)
    for i in range(4):
        for iy in range(8):
            mix_ref[place_of_register(i, iy), :] = (1.0 - frac[i][iy]) / boxed[i][iy]


def interior_kernel(with_speed, u_ref, frac_ref, res_ref, prim_ref, wx_ref):
    interior_body(u_ref, frac_ref, res_ref, prim_ref, wx_ref, with_speed)


def update_kernel(count, first, *refs):
    base_ref, frac_ref, mix_ref, inner_ref = refs[0:4]
    own_refs, ghost_refs = refs[4:10], refs[10:16]
    refs = refs[16:]
    if first:
        new_ref, message_refs, faces_ref, res_ref = refs[0], refs[1:7], refs[7], refs[8]
    else:
        faces_ref, new_ref, message_refs, res_ref = refs[0], refs[1], refs[2:8], refs[8]
    _, even, far = cube_place(count)
    res_ref[...] = inner_ref[...]

    def aperture_of(direction, other):
        number = 2 * direction + other
        if not first:
            return faces_ref[number]
        own, ghost = own_refs[number][5], ghost_refs[number][5]
        if other == 1 and far[direction] is not None:
            ghost = jnp.where(far[direction], own, ghost)
        aperture = jnp.minimum(own, ghost)
        faces_ref[number] = aperture
        return aperture

    boundary_body(res_ref, aperture_of, own_refs, ghost_refs, even, far, True)
    for register in range(32):
        at = pl.ds(register * 8, 8)
        scale = frac_ref[at, :] * (-CFL_NUMBER / res_ref[5, at, :])
        for q in range(5):
            res_ref[q, at, :] = res_ref[q, at, :] * scale
    factor = FIRST_SECTION if first else 1.0
    for q in range(5):
        share = [[res_ref[q, place_of_register(i, iy), :] for iy in range(8)] for i in range(4)]
        boxed = box_sum(share)
        for i in range(4):
            for iy in range(8):
                at = place_of_register(i, iy)
                mixed = share[i][iy] + mix_ref[at, :] * boxed[i][iy]
                if first:
                    mixed = factor * mixed
                new_ref[q, at, :] = base_ref[q, at, :] + mixed
    write_messages([(new_ref, (q,)) for q in range(5)], message_refs, even)


def coarse_rows(registers, order3, rows_ref, half_ref):
    for i in (0, 1):
        for jy in range(4):
            half_ref[pl.ds((i * 4 + jy) * 8, 8), :] = (
                registers(2 * i, 2 * jy)
                + registers(2 * i, 2 * jy + 1)
                + registers(2 * i + 1, 2 * jy)
                + registers(2 * i + 1, 2 * jy + 1)
            )
    for i in (0, 1):
        for jy in range(4):
            start = (i * 4 + jy) * 8
            rows_ref[pl.ds(i * 64 + jy * 8, 4), :] = (
                half_ref[pl.ds(start, 4, stride=2), :] + half_ref[pl.ds(start + 1, 4, stride=2), :]
            )
    parts = jnp.concatenate(split3(rows_ref[...]), axis=1)
    placed = lax.dot_general(order3, parts, (((1,), (1,)), ((), ())), preferred_element_type=F32)
    tiles = []
    for tile in range(4):
        total = None
        for number in range(4):
            start = (tile * 4 + number) * 8
            piece = turn(placed[start : start + 8, :], (number // 2) * 32 + (number % 2) * 4, 1)
            total = piece if total is None else total + piece
        tiles.append(total)
    return jnp.concatenate(tiles, axis=1)


def tripled_order(order_ref):
    order = order_ref[...].astype(BF16)
    return jnp.concatenate([order, order, order], axis=1)


def state_kernel(u_ref, frac_ref, order_ref, kept_ref, sent_ref, rows_ref, half_ref):
    rows_ref[...] = jnp.zeros_like(rows_ref)
    order3 = tripled_order(order_ref)
    for q in range(6):
        if q < 5:
            def registers(i, iy, q=q):
                at = place_of_register(i, iy)
                return frac_ref[at, :] * u_ref[q, at, :]
        else:
            def registers(i, iy):
                return frac_ref[place_of_register(i, iy), :]
        sums = coarse_rows(registers, order3, rows_ref, half_ref)
        kept_ref[q] = sums[0:4]
        sent_ref[q] = sums[4:8]


def output_kernel(u_ref, spread_ref, out_ref):
    tripled = []
    for half in (0, 1):
        spread = spread_ref[half].astype(BF16)
        tripled.append(jnp.concatenate([spread, spread, spread], axis=1))
    dims = (((1,), (1,)), ((), ()))
    for q in range(5):
        parts = jnp.concatenate(split3(u_ref[q]), axis=1)
        for half in (0, 1):
            out_ref[q, :, pl.ds(half * 256, 256)] = lax.dot_general(
                tripled[half], parts, dims, preferred_element_type=F32
            )


def residual_kernel(count, *refs):
    inner_ref, faces_ref, order_ref, sent_state_ref = refs[0:4]
    own_refs, ghost_refs = refs[4:10], refs[10:16]
    kept_ref, sent_ref, res_ref, rows_ref, half_ref = refs[16:21]
    _, even, far = cube_place(count)
    res_ref[...] = inner_ref[...]
    boundary_body(
        res_ref,
        lambda direction, other: faces_ref[2 * direction + other],
        own_refs,
        ghost_refs,
        even,
        far,
        False,
    )
    rows_ref[...] = jnp.zeros_like(rows_ref)
    order3 = tripled_order(order_ref)
    for q in range(5):
        sums = coarse_rows(
            lambda i, iy: res_ref[q, place_of_register(i, iy), :], order3, rows_ref, half_ref
        )
        kept_ref[q] = sums[0:4]
        sent_ref[6 + q] = sums[4:8]
    sent_ref[0:6] = sent_state_ref[...]


def coarse_kernel(pick_ref, kept_state_ref, kept_res_ref, got_ref, out_state_ref, out_res_ref):
    pick = pick_ref[...]
    chosen = [jnp.broadcast_to(pick[:, source : source + 1], (8, 512)) > 0.5 for source in range(8)]

    def choose(kept, received):
        result = None
        for source in range(8):
            row = kept[source : source + 1] if source < 4 else received[source - 4 : source - 3]
            row = jnp.broadcast_to(row, (8, 512))
            result = row if result is None else jnp.where(chosen[source], row, result)
        return result

    weight = choose(kept_state_ref[5], got_ref[5])
    for q in range(5):
        out_state_ref[q] = choose(kept_state_ref[q], got_ref[q]) / weight
        out_res_ref[q] = choose(kept_res_ref[q], got_ref[6 + q])


def f32(*shape):
    return jax.ShapeDtypeStruct(shape, F32)


def held(*shape):
    return pltpu.VMEM(shape, F32)


def call(kernel, outs, scratch, args, sources=0):
    vmem = pl.BlockSpec(memory_space=pltpu.VMEM)
    spaces = [pltpu.HBM] * sources + [pltpu.VMEM] * (len(args) - sources)
    args = [pltpu.with_memory_space_constraint(arg, space) for arg, space in zip(args, spaces)]
    return pl.pallas_call(
        kernel,
        out_shape=outs,
        in_specs=[pl.BlockSpec(memory_space=space) for space in spaces],
        out_specs=[vmem] * len(outs),
        scratch_shapes=[pltpu.VMEM(item, F32) if isinstance(item, tuple) else item for item in scratch],
        compiler_params=pltpu.CompilerParams(vmem_limit_bytes=8 << 20),
        cost_estimate=pl.CostEstimate(flops=8_000_000, bytes_accessed=4_000_000, transcendentals=0),
    )(*args)


START_ORDER = (3, 1, 4, 5, 2, 0)


def solution(mesh):
    count = mesh.shape[AXIS]
    swaps = pair_swaps(count)
    forward = [(device, (device + 1) % count) for device in range(count)]

    def exchange(messages):
        ghosts = [None] * 6
        for number in START_ORDER:
            ghosts[number] = lax.ppermute(messages[number], AXIS, swaps[number])
        return ghosts

    def interior(u, frac, with_speed):
        rows = 6 if with_speed else 5
        return call(
            lambda *refs: interior_kernel(with_speed, *refs),
            [held(rows, ROWS, LANES)],
            [(5, ROWS, LANES), (rows, 64, LANES)],
            [u, frac],
        )[0]

    def local(state, volume, neighbour, parent):
        parent = parent.reshape(1, 64)
        neighbour = neighbour.T
        grid = held(5, ROWS, LANES)
        u, frac, *sent = call(
            lambda *refs: prepare_kernel(count, *refs),
            [grid, held(ROWS, LANES)] + [held(6, 8, LANES)] * 6,
            [
                (5, 64, 512),
                pltpu.VMEM((64, 512), I32),
                pltpu.VMEM((6, 64), I32),
                pltpu.VMEM((1, 64), I32),
                pltpu.SemaphoreType.DMA((8,)),
            ],
            [state, volume, neighbour, parent],
            4,
        )
        ghosts = exchange(sent)
        spread, order, pick = call(
            tables_kernel,
            [held(2, 64, LANES), held(LANES, LANES), held(8, LANES)],
            [],
            [neighbour, parent],
        )
        mix = call(mixing_kernel, [held(ROWS, LANES)], [], [frac])[0]
        inner = interior(u, frac, True)
        middle, *rest = call(
            lambda *refs: update_kernel(count, True, *refs),
            [grid] + [held(5, 8, LANES)] * 6 + [held(6, 8, LANES)],
            [(6, ROWS, LANES)],
            [u, frac, mix, inner, *sent, *ghosts],
        )
        sent, faces = rest[0:6], rest[6]
        ghosts = exchange(sent)
        inner = interior(middle, frac, True)
        fine, *sent = call(
            lambda *refs: update_kernel(count, False, *refs),
            [grid] + [held(5, 8, LANES)] * 6,
            [(6, ROWS, LANES)],
            [u, frac, mix, inner, *sent, *ghosts, faces],
        )
        ghosts = exchange(sent)
        inner = interior(fine, frac, False)
        kept_state, sent_state = call(
            state_kernel,
            [held(6, 4, 512), held(6, 4, 512)],
            [(LANES, LANES), (64, LANES)],
            [fine, frac, order],
        )
        kept_res, outgoing = call(
            lambda *refs: residual_kernel(count, *refs),
            [held(5, 4, 512), held(11, 4, 512)],
            [(5, ROWS, LANES), (LANES, LANES), (64, LANES)],
            [inner, faces, order, sent_state, *sent, *ghosts],
        )
        got = lax.ppermute(outgoing, AXIS, forward)
        fine_out = call(output_kernel, [f32(5, 64, 512)], [], [fine, spread])[0]
        coarse_state, coarse_residual = call(
            coarse_kernel, [f32(5, 8, 512), f32(5, 8, 512)], [], [pick, kept_state, kept_res, got]
        )
        return fine_out, coarse_state, coarse_residual

    in_specs = (P(None, AXIS, None), P(AXIS, None), P(AXIS, None), P(AXIS))
    out_specs = (P(None, AXIS, None), P(None, AXIS, None), P(None, AXIS, None))
    return jax.shard_map(local, mesh=mesh, in_specs=in_specs, out_specs=out_specs, check_vma=False)
```
